32 devices in a mesh: geom: 2 (over x), op: 8 (over z, y), col: 2 (over core).
Axes of the slice: x: 2, y: 2, z: 4, core: 2. Of those that a mesh axis runs over, the one named last changes fastest.
Arguments:
- wave_coef: float32 [2048, 1024], P('geom', 'col'), parts along dimension 0, may hold values from -6 to 6
- diag_energy: float32 [2048, 1024], P('geom', 'col'), parts along dimension 0, may hold values from -4 to 4
- left_block: bfloat16 [32, 1024, 1024], P(('geom', 'op')), parts along dimension 0, may hold values from -0.1875 to 0.1875
- right_block: bfloat16 [32, 1024, 1024], P(('geom', 'op'), None, 'col'), parts along dimension 0, may hold values from -0.1875 to 0.1875
- block_mask: int32 [32, 8, 8], P(('geom', 'op')), parts along dimension 0, may hold values 0 or 1
Outputs:
- new_wave: float32 [2048, 1024], P('geom', 'col'), parts along dimension 0
The draws below stay inside these ranges and needn't reach their ends.
There are 2 independent parts, one for each index of `geom`. The reference program is written for one: setup_inputs(seed, part) draws one part's arguments, and reference() takes and returns one part's arrays. A program takes and returns all parts, laid end to end along the dimension named above; each array names one. Nothing has to cross between parts.
All inputs are finite; a program needn't handle non-finite values. No bound on the sum of `block_mask` on one device may be relied on, other than what follows from the above.
Results may differ from the reference program's by a relative error of at most 0.0042.
The reference program's roundings to bfloat16 on the way (of `masked`, `wave` and `inner`) count: a program that leaves them out, or rounds other values in their place, can miss the bound.
Values may be sent and summed in bfloat16 or wider, within the bound.
A program may use at most 64 MiB of HBM per device.

```python
import jax
import jax.numpy as jnp
from jax import lax

M = 1024
NB = 8
STEPS = 2
PAIRS = 16


def plant(entries, key, low, top_value):
    spot = [jax.random.randint(jax.random.fold_in(key, axis), (), 0, length) for axis, length in enumerate(entries.shape)]
    main_axis = entries.shape.index(max(entries.shape))
    neighbour = spot[:main_axis] + [(spot[main_axis] + 1) % entries.shape[main_axis]] + spot[main_axis + 1:]
    return entries.at[tuple(spot)].set(low).at[tuple(neighbour)].set(top_value)


def block_levels(stream_key, shape, shards, smallest, largest):
    gain, own = 1.0, jax.random.fold_in(stream_key, 6)
    for position, parts in shards:
        steps = jnp.exp(jax.random.uniform(jax.random.fold_in(own, position), (parts,), jnp.float32, smallest / len(shards), largest / len(shards)))
        gain = gain * jnp.repeat(steps, shape[position] // parts).reshape([-1 if axis == position else 1 for axis in range(len(shape))])
    return gain


def normal_values(own_key, dims, scale, bound, shards=(), held_as=jnp.bfloat16):
    drawn = scale * jax.random.normal(own_key, dims, jnp.float32)
    if shards:
        drawn = drawn * block_levels(own_key, dims, shards, -0.22, 0.18)
    return jnp.clip(drawn, -bound, bound).astype(held_as)


def setup_inputs(seed: int = 0, part: int = 0) -> dict:
    splits = jax.random.split(jax.random.key(seed), 6)
    own_keys = jax.random.split(jax.random.fold_in(splits[5], part), 6)
    return {
        "wave_coef": normal_values(own_keys[0], (M, M), 1.0, 6.0, ((1, 2),), jnp.float32),
        "diag_energy": jnp.clip(jax.random.uniform(own_keys[1], (M, M), jnp.float32, -4.0, 4.0) * block_levels(own_keys[1], (M, M), ((1, 2),), -0.4, 0.0), -4.0, 4.0),
        "left_block": normal_values(own_keys[2], (PAIRS, M, M), M ** -0.5, 0.1875, ((0, 8),)),
        "right_block": normal_values(own_keys[3], (PAIRS, M, M), M ** -0.5, 0.1875, ((0, 8), (2, 2))),
        "block_mask": plant((jax.random.randint(own_keys[4], (PAIRS, NB, NB), 0, 2) < 1).astype(jnp.int32), jax.random.fold_in(own_keys[4], 1), 0, 1),
    }


def apply_mask(left_block, block_mask):
    total, width, _ = left_block.shape
    blocks = block_mask.shape[1]
    inside = width // blocks
    grid = left_block.reshape(total, blocks, inside, blocks, inside)
    keep = block_mask.astype(jnp.bfloat16)[:, :, None, :, None]
    return (grid * keep).reshape(total, width, width)

def update(coef, sigma, diag_energy):
    theta = jnp.mean(coef * sigma) / (jnp.mean(coef * coef) + 1e-06)
    spacing = diag_energy - theta
    correction = (sigma - theta * coef) * spacing / jnp.maximum(spacing * spacing, 1.0)
    moved = coef - correction
    return moved * lax.rsqrt(jnp.mean(moved * moved) + 1e-06)

def reference(wave_coef, diag_energy, left_block, right_block, block_mask):
    masked = apply_mask(left_block, block_mask)
    coef = wave_coef
    for step in range(STEPS):
        wave = coef.astype(jnp.bfloat16)

        def add_pair(total, operands):
            left_op, right_op = operands
            inner = jnp.dot(wave, right_op, preferred_element_type=jnp.float32).astype(jnp.bfloat16)
            return (total + jnp.dot(left_op, inner, preferred_element_type=jnp.float32), None)
        sigma, _ = lax.scan(add_pair, jnp.zeros(coef.shape, jnp.float32), (masked, right_block))
        coef = update(coef, sigma, diag_energy)
    return coef
```

```python
import functools

import jax
import jax.numpy as jnp
from jax import lax
from jax.experimental import pallas as pl
from jax.experimental.pallas import tpu as pltpu
from jax.sharding import PartitionSpec as P

STEPS = 2
MESH = pl.DeviceIdType.MESH
F32 = jnp.float32
BF16 = jnp.bfloat16


def fold(total):
    return sum(total[:, i:i + 128] for i in range(0, total.shape[1], 128))


def whole(total):
    return jnp.sum(jnp.sum(total, axis=1, keepdims=True), axis=0, keepdims=True)


def rows8(product):
    return product.reshape(product.shape[0] // 8, 8, product.shape[1]).sum(0)


def kernel(
    groups, cells, wave_parts, tile,
    coef_hbm, diag_hbm, left_hbm, right_hbm, mask_ref,
    out_ref, norm_ref,
    coef, diag, left, right, masked, inner, wave_own, wave_other,
    own, y_out, y_in, z_out, z_in, sig, scal_out, scal_in,
    load_sem, wave_sem, y_sem, z_sem, zg_sem, yg_sem, scal_sem,
):
    op, col = lax.axis_index("op"), lax.axis_index("col")
    a, h = op // 2, lax.rem(op, 2)
    mate = a * 2 + 1 - h
    other = 1 - col
    width, cols = coef.shape
    pairs = left.shape[0]
    rows = width // (2 * groups)
    blocks = mask_ref.shape[1]
    inside = width // blocks

    loads = [
        pltpu.make_async_copy(src, dst, load_sem.at[i])
        for i, (src, dst) in enumerate(
            ((coef_hbm, coef), (right_hbm, right), (left_hbm, left), (diag_hbm, diag))
        )
    ]
    for load in loads:
        load.start()

    barrier = pltpu.get_barrier_semaphore()
    peers = [{"col": other}, {"op": mate}]
    peers += [{"op": lax.rem(a + 1 + j, groups) * 2 + h} for j in range(groups - 1)]
    for peer in peers:
        pl.semaphore_signal(barrier, inc=1, device_id=peer, device_id_type=MESH)
    loads[0].wait()
    pl.semaphore_wait(barrier, len(peers))

    started = []

    def send(src, dst, sems, device_id):
        copy = pltpu.make_async_remote_copy(
            src_ref=src, dst_ref=dst, send_sem=sems[0], recv_sem=sems[1],
            device_id=device_id, device_id_type=MESH,
        )
        copy.start()
        started.append(copy)
        return copy

    def at(index):
        return pl.ds(pl.multiple_of(index * rows, rows), rows)

    def share(step, event, totals):
        for i, total in enumerate(totals):
            scal_out[step, event, i] = fold(total)
        copy = send(
            scal_out.at[step, event], scal_in.at[step, event],
            (scal_sem.at[0, step, event], scal_sem.at[1, step, event]), {"col": other},
        )
        copy.wait_recv()
        return [whole(scal_out[step, event, i] + scal_in[step, event, i]) for i in range(len(totals))]

    zero = jnp.zeros((8, cols), F32)
    scale = None
    for step in range(STEPS):
        part = width // wave_parts
        wave_copies = []
        for r in range(wave_parts):
            span = pl.ds(r * part, part)
            value = coef[span, :]
            if scale is not None:
                value = value * scale
                coef[span, :] = value
            wave_own[step, span, :] = value.astype(BF16)
            wave_copies.append(send(
                wave_own.at[step, span], wave_other.at[step, span],
                (wave_sem.at[0, step, r], wave_sem.at[1, step, r]), {"col": other},
            ))
        if step == 0:
            loads[1].wait()
        mine = pl.ds(pl.multiple_of(col * cols, cols), cols)
        theirs = pl.ds(pl.multiple_of(other * cols, cols), cols)
        for r in range(wave_parts):
            span = pl.ds(r * part, part)
            wave_copies[r].wait_recv()
            for k in range(pairs):
                value = jnp.dot(wave_own[step, span, :], right[k, mine, :], preferred_element_type=F32)
                value += jnp.dot(wave_other[step, span, :], right[k, theirs, :], preferred_element_type=F32)
                inner[pl.ds(k * width + r * part, part), :] = value.astype(BF16)
        if step == 0:
            loads[2].wait()

            def mask_rows(i, carry):
                span = pl.ds(pl.multiple_of(i * inside, inside), inside)
                for k in range(pairs):
                    for j in range(blocks):
                        keep = jnp.full((inside, inside), mask_ref[k, i, j].astype(F32)).astype(BF16)
                        masked[span, k * width + j * inside:k * width + (j + 1) * inside] = (
                            left[k, span, j * inside:(j + 1) * inside] * keep
                        )
                return carry

            lax.fori_loop(0, blocks, mask_rows, 0)

        to_mate = []
        for j in range(groups):
            target = lax.rem(a + 1 + j, groups)
            span = pl.ds(pl.multiple_of(target * 2 * rows, 2 * rows), 2 * rows)
            value = jnp.dot(masked[span, :], inner[...], preferred_element_type=F32)
            low, high = value[:rows], value[rows:]
            y_out[step, j] = jnp.where(h == 0, high, low).astype(BF16)
            to_mate.append(send(
                y_out.at[step, j], y_in.at[step, j],
                (y_sem.at[0, step, j], y_sem.at[1, step, j]), {"op": mate},
            ))
            own[j] = jnp.where(h == 0, low, high)

        if step == 0:
            loads[3].wait()

        def weigh(i, acc):
            value = coef[pl.ds(pl.multiple_of(i * tile, tile), tile), :]
            return acc + rows8(value * value)

        weight = lax.fori_loop(0, width // tile, weigh, zero)

        to_group = []
        for j in range(groups):
            to_mate[j].wait_recv()
            value = own[j] + y_in[step, j].astype(F32)
            if j < groups - 1:
                z_out[step, j] = value.astype(BF16)
                to_group.append(send(
                    z_out.at[step, j], z_in.at[step, j],
                    (z_sem.at[0, step, j], z_sem.at[1, step, j]),
                    {"op": lax.rem(a + 1 + j, groups) * 2 + h},
                ))
        for j in range(groups - 1):
            to_group[j].wait_recv()
            value = value + z_in[step, j].astype(F32)
        sig[step, at(op), :] = value.astype(BF16)

        to_mate = [send(
            sig.at[step, at(op)], sig.at[step, at(op)],
            (yg_sem.at[0, step, groups - 1], yg_sem.at[1, step, groups - 1]), {"op": mate},
        )]
        to_group = [
            send(
                sig.at[step, at(op)], sig.at[step, at(op)],
                (zg_sem.at[0, step, j], zg_sem.at[1, step, j]),
                {"op": lax.rem(a + 1 + j, groups) * 2 + h},
            )
            for j in range(groups - 1)
        ]

        def correlate(index, acc):
            return acc + rows8(coef[at(index), :] * sig[step, at(index), :].astype(F32))

        correlation = correlate(op, zero)
        for j in range(groups - 1):
            to_group[j].wait_recv()
            source = lax.rem(a + groups - 1 - j, groups)
            arrived = at(source * 2 + h)
            to_mate.append(send(
                sig.at[step, arrived], sig.at[step, arrived],
                (yg_sem.at[0, step, j], yg_sem.at[1, step, j]), {"op": mate},
            ))
            correlation = correlate(source * 2 + h, correlation)
        to_mate[0].wait_recv()
        correlation = correlate(mate, correlation)
        for j in range(groups - 1):
            to_mate[1 + j].wait_recv()
            source = lax.rem(a + groups - 1 - j, groups)
            correlation = correlate(source * 2 + 1 - h, correlation)

        total, weight = share(step, 0, [correlation, weight])
        theta = total / cells / (weight / cells + 1e-06)
        target_ref = coef if step < STEPS - 1 else out_ref

        def move(i, acc):
            span = pl.ds(pl.multiple_of(i * tile, tile), tile)
            value = coef[span, :]
            spacing = diag[span, :] - theta
            correction = (sig[step, span, :].astype(F32) - theta * value) * spacing / jnp.maximum(spacing * spacing, 1.0)
            moved = value - correction
            target_ref[span, :] = moved
            return acc + rows8(moved * moved)

        norm = lax.fori_loop(0, width // tile, move, zero)
        (norm,) = share(step, 1, [norm])
        scale = lax.rsqrt(norm / cells + 1e-06)

    norm_ref[...] = jnp.broadcast_to(scale, norm_ref.shape)
    for copy in started:
        copy.wait_send()


def local(groups, sides, wave_coef, diag_energy, left_block, right_block, block_mask):
    width, cols = wave_coef.shape
    pairs = left_block.shape[0]
    rows = width // (2 * groups)
    parts = 4
    dma = pltpu.SemaphoreType.DMA
    vmem = pltpu.VMEM
    moved, scale = pl.pallas_call(
        functools.partial(kernel, groups, float(width * cols * sides), parts, 32),
        out_shape=(
            jax.ShapeDtypeStruct((width, cols), F32),
            jax.ShapeDtypeStruct((8, 128), F32),
        ),
        in_specs=[pl.BlockSpec(memory_space=pl.ANY)] * 4 + [pl.BlockSpec(memory_space=pltpu.SMEM)],
        out_specs=(pl.BlockSpec(memory_space=vmem), pl.BlockSpec(memory_space=vmem)),
        scratch_shapes=[
            vmem((width, cols), F32),
            vmem((width, cols), F32),
            vmem(left_block.shape, BF16),
            vmem(right_block.shape, BF16),
            vmem((width, pairs * width), BF16),
            vmem((pairs * width, cols), BF16),
            vmem((STEPS, width, cols), BF16),
            vmem((STEPS, width, cols), BF16),
            vmem((groups, rows, cols), F32),
            vmem((STEPS, groups, rows, cols), BF16),
            vmem((STEPS, groups, rows, cols), BF16),
            vmem((STEPS, groups - 1, rows, cols), BF16),
            vmem((STEPS, groups - 1, rows, cols), BF16),
            vmem((STEPS, width, cols), BF16),
            vmem((STEPS, 2, 2, 8, 128), F32),
            vmem((STEPS, 2, 2, 8, 128), F32),
            dma((4,)),
            dma((2, STEPS, parts)),
            dma((2, STEPS, groups)),
            dma((2, STEPS, groups - 1)),
            dma((2, STEPS, groups - 1)),
            dma((2, STEPS, groups)),
            dma((2, STEPS, 2)),
        ],
        compiler_params=pltpu.CompilerParams(
            collective_id=0, has_side_effects=True, vmem_limit_bytes=60 * 1024 * 1024
        ),
    )(wave_coef, diag_energy, left_block, right_block, block_mask)
    return moved * scale[0, 0]


def solution(mesh):
    in_specs = (
        P("geom", "col"),
        P("geom", "col"),
        P(("geom", "op"), None, None),
        P(("geom", "op"), None, "col"),
        P(("geom", "op"), None, None),
    )
    return jax.shard_map(
        functools.partial(local, mesh.shape["op"] // 2, mesh.shape["col"]),
        mesh=mesh, in_specs=in_specs, out_specs=P("geom", "col"), check_vma=False,
    )
```

```python
import functools

import jax
import jax.numpy as jnp
from jax import lax
from jax.experimental import pallas as pl
from jax.experimental.pallas import tpu as pltpu
from jax.sharding import PartitionSpec as P

STEPS = 2
MESH = pl.DeviceIdType.MESH
F32 = jnp.float32
BF16 = jnp.bfloat16


def fold(total):
    return sum(total[:, i:i + 128] for i in range(0, total.shape[1], 128))


def whole(total):
    return jnp.sum(jnp.sum(total, axis=1, keepdims=True), axis=0, keepdims=True)


def rows8(product):
    return product.reshape(product.shape[0] // 8, 8, product.shape[1]).sum(0)


def kernel(
    groups, cells, wave_parts, tile,
    coef_hbm, diag_hbm, left_hbm, right_hbm, mask_ref,
    out_ref, norm_ref,
    coef, diag, left, right, masked, inner, wave_own, wave_other,
    own, y_out, y_in, z_out, z_in, sig, scal_out, scal_in,
    load_sem, wave_sem, y_sem, z_sem, zg_sem, yg_sem, scal_sem,
):
    op, col = lax.axis_index("op"), lax.axis_index("col")
    a, h = op // 2, lax.rem(op, 2)
    mate = a * 2 + 1 - h
    other = 1 - col
    width, cols = coef.shape
    pairs = left.shape[0]
    rows = width // (2 * groups)
    bands, band = inner.shape[0], inner.shape[2]
    blocks = mask_ref.shape[1]
    inside = width // blocks

    loads = [
        pltpu.make_async_copy(src, dst, load_sem.at[i])
        for i, (src, dst) in enumerate(
            ((coef_hbm, coef), (right_hbm, right), (left_hbm, left), (diag_hbm, diag))
        )
    ]
    for load in loads[:2]:
        load.start()

    barrier = pltpu.get_barrier_semaphore()
    peers = [{"col": other}, {"op": mate}]
    peers += [{"op": lax.rem(a + 1 + j, groups) * 2 + h} for j in range(groups - 1)]
    for peer in peers:
        pl.semaphore_signal(barrier, inc=1, device_id=peer, device_id_type=MESH)
    loads[0].wait()
    for load in loads[2:]:
        load.start()
    pl.semaphore_wait(barrier, len(peers))

    started = []

    def send(src, dst, sems, device_id):
        copy = pltpu.make_async_remote_copy(
            src_ref=src, dst_ref=dst, send_sem=sems[0], recv_sem=sems[1],
            device_id=device_id, device_id_type=MESH,
        )
        copy.start()
        started.append(copy)
        return copy

    def at(index):
        return pl.ds(pl.multiple_of(index * rows, rows), rows)

    def share(step, event, totals):
        for i, total in enumerate(totals):
            scal_out[step, event, i] = fold(total)
        copy = send(
            scal_out.at[step, event], scal_in.at[step, event],
            (scal_sem.at[0, step, event], scal_sem.at[1, step, event]), {"col": other},
        )
        copy.wait_recv()
        return [whole(scal_out[step, event, i] + scal_in[step, event, i]) for i in range(len(totals))]

    hops = (groups // 2, groups - 1 - groups // 2)
    legs = [(way, t) for t in range(hops[0]) for way in range(2) if t < hops[way]]

    def origin(way, t):
        return lax.rem(a + (groups - 1 - t if way == 0 else 1 + t), groups)

    zero = jnp.zeros((8, cols), F32)
    scale = None
    for step in range(STEPS):
        part = width // wave_parts
        wave_copies = []
        for r in range(wave_parts):
            span = pl.ds(r * part, part)
            value = coef[span, :]
            if scale is not None:
                value = value * scale
                coef[span, :] = value
            wave_own[step, span, :] = value.astype(BF16)
            wave_copies.append(send(
                wave_own.at[step, span], wave_other.at[step, span],
                (wave_sem.at[0, step, r], wave_sem.at[1, step, r]), {"col": other},
            ))
        if step == 0:
            loads[1].wait()
        mine = pl.ds(pl.multiple_of(col * cols, cols), cols)
        theirs = pl.ds(pl.multiple_of(other * cols, cols), cols)
        state = {"corr": jnp.zeros((8, band), F32)}
        mate_in, group_in, mate_back, group_back = {}, {}, {}, {}

        def contract(b):
            lanes = slice(b * band, (b + 1) * band)
            for r in range(wave_parts):
                span = pl.ds(r * part, part)
                if b == 0:
                    wave_copies[r].wait_recv()
                for k in range(pairs):
                    value = jnp.dot(wave_own[step, span, :], right[k, mine, lanes], preferred_element_type=F32)
                    value += jnp.dot(wave_other[step, span, :], right[k, theirs, lanes], preferred_element_type=F32)
                    inner[b, pl.ds(k * width + r * part, part), :] = value.astype(BF16)

        def apply_mask():
            loads[2].wait()

            def mask_rows(i, carry):
                span = pl.ds(pl.multiple_of(i * inside, inside), inside)
                for k in range(pairs):
                    for j in range(blocks):
                        keep = jnp.full((inside, inside), mask_ref[k, i, j].astype(F32)).astype(BF16)
                        masked[span, k * width + j * inside:k * width + (j + 1) * inside] = (
                            left[k, span, j * inside:(j + 1) * inside] * keep
                        )
                return carry

            lax.fori_loop(0, blocks, mask_rows, 0)

        def halves(b):
            mate_in[b] = []
            for j in range(groups):
                target = lax.rem(a + 1 + j, groups)
                span = pl.ds(pl.multiple_of(target * 2 * rows, 2 * rows), 2 * rows)
                value = jnp.dot(masked[span, :], inner[b], preferred_element_type=F32)
                low, high = value[:rows], value[rows:]
                y_out[step, b, j] = jnp.where(h == 0, high, low).astype(BF16)
                mate_in[b].append(send(
                    y_out.at[step, b, j], y_in.at[step, b, j],
                    (y_sem.at[0, step, b, j], y_sem.at[1, step, b, j]), {"op": mate},
                ))
                own[b, j] = jnp.where(h == 0, low, high)

        def to_owner(b):
            group_in[b] = []
            for j in range(groups):
                mate_in[b][j].wait_recv()
                value = own[b, j] + y_in[step, b, j].astype(F32)
                if j < groups - 1:
                    z_out[step, b, j] = value.astype(BF16)
                    group_in[b].append(send(
                        z_out.at[step, b, j], z_in.at[step, b, j],
                        (z_sem.at[0, step, b, j], z_sem.at[1, step, b, j]),
                        {"op": lax.rem(a + 1 + j, groups) * 2 + h},
                    ))
                else:
                    own[b, j] = value

        def correlate(b, index):
            lanes = slice(b * band, (b + 1) * band)
            state["corr"] += rows8(coef[at(index), lanes] * sig[step, b, at(index), :].astype(F32))

        def relay(b, way, t, source):
            chunk = sig.at[step, b, at(source)]
            slot = way * hops[0] + t
            group_back[b, way, t] = send(
                chunk, chunk, (zg_sem.at[0, step, b, slot], zg_sem.at[1, step, b, slot]),
                {"op": lax.rem(a + (1 if way == 0 else groups - 1), groups) * 2 + h},
            )

        def finish(b):
            value = own[b, groups - 1]
            for j in range(groups - 1):
                group_in[b][j].wait_recv()
                value = value + z_in[step, b, j].astype(F32)
            sig[step, b, at(op), :] = value.astype(BF16)
            chunk = sig.at[step, b, at(op)]
            for way, length in enumerate(hops):
                if length:
                    relay(b, way, 0, op)
            mate_back[b] = [send(
                chunk, chunk,
                (yg_sem.at[0, step, b, groups - 1], yg_sem.at[1, step, b, groups - 1]), {"op": mate},
            )]
            correlate(b, op)

        def forward(b):
            for way, t in legs:
                group_back[b, way, t].wait_recv()
                source = origin(way, t) * 2 + h
                if t + 1 < hops[way]:
                    relay(b, way, t + 1, source)
                chunk = sig.at[step, b, at(source)]
                slot = way * hops[0] + t
                mate_back[b].append(send(
                    chunk, chunk, (yg_sem.at[0, step, b, slot], yg_sem.at[1, step, b, slot]), {"op": mate},
                ))
                correlate(b, source)

        def collect(b):
            mate_back[b][0].wait_recv()
            correlate(b, mate)
            for i, (way, t) in enumerate(legs):
                mate_back[b][1 + i].wait_recv()
                correlate(b, origin(way, t) * 2 + 1 - h)

        for b in range(bands):
            contract(b)
            if step == 0 and b == 0:
                apply_mask()
            halves(b)
        if step == 0:
            loads[3].wait()

        def weigh(i, acc):
            value = coef[pl.ds(pl.multiple_of(i * tile, tile), tile), :]
            return acc + rows8(value * value)

        weight = lax.fori_loop(0, width // tile, weigh, zero)
        for b in range(bands):
            to_owner(b)
            if b > 0:
                forward(b - 1)
            finish(b)
            if b > 0:
                collect(b - 1)
        forward(bands - 1)
        collect(bands - 1)
        correlation = state["corr"]

        total, weight = share(step, 0, [correlation, weight])
        theta = total / cells / (weight / cells + 1e-06)
        target_ref = coef if step < STEPS - 1 else out_ref

        def move(i, acc):
            span = pl.ds(pl.multiple_of(i * tile, tile), tile)
            value = coef[span, :]
            spacing = diag[span, :] - theta
            sigma = jnp.concatenate([sig[step, b, span, :] for b in range(bands)], axis=1).astype(F32)
            correction = (sigma - theta * value) * spacing * pl.reciprocal(jnp.maximum(spacing * spacing, 1.0))
            moved = value - correction
            target_ref[span, :] = moved
            return acc + rows8(moved * moved)

        norm = lax.fori_loop(0, width // tile, move, zero)
        (norm,) = share(step, 1, [norm])
        scale = lax.rsqrt(norm / cells + 1e-06)

    norm_ref[...] = jnp.broadcast_to(scale, norm_ref.shape)
    for copy in started:
        copy.wait_send()


def local(groups, sides, wave_coef, diag_energy, left_block, right_block, block_mask):
    width, cols = wave_coef.shape
    pairs = left_block.shape[0]
    rows = width // (2 * groups)
    parts = 4
    bands = max(1, cols // 256)
    band = cols // bands
    dma = pltpu.SemaphoreType.DMA
    vmem = pltpu.VMEM
    moved, scale = pl.pallas_call(
        functools.partial(kernel, groups, float(width * cols * sides), parts, 32),
        out_shape=(
            jax.ShapeDtypeStruct((width, cols), F32),
            jax.ShapeDtypeStruct((8, cols), F32),
        ),
        in_specs=[pl.BlockSpec(memory_space=pl.ANY)] * 4 + [pl.BlockSpec(memory_space=pltpu.SMEM)],
        out_specs=(pl.BlockSpec(memory_space=vmem), pl.BlockSpec(memory_space=vmem)),
        scratch_shapes=[
            vmem((width, cols), F32),
            vmem((width, cols), F32),
            vmem(left_block.shape, BF16),
            vmem(right_block.shape, BF16),
            vmem((width, pairs * width), BF16),
            vmem((bands, pairs * width, band), BF16),
            vmem((STEPS, width, cols), BF16),
            vmem((STEPS, width, cols), BF16),
            vmem((bands, groups, rows, band), F32),
            vmem((STEPS, bands, groups, rows, band), BF16),
            vmem((STEPS, bands, groups, rows, band), BF16),
            vmem((STEPS, bands, groups - 1, rows, band), BF16),
            vmem((STEPS, bands, groups - 1, rows, band), BF16),
            vmem((STEPS, bands, width, band), BF16),
            vmem((STEPS, 2, 2, 8, 128), F32),
            vmem((STEPS, 2, 2, 8, 128), F32),
            dma((4,)),
            dma((2, STEPS, parts)),
            dma((2, STEPS, bands, groups)),
            dma((2, STEPS, bands, groups - 1)),
            dma((2, STEPS, bands, groups - 1)),
            dma((2, STEPS, bands, groups)),
            dma((2, STEPS, 2)),
        ],
        compiler_params=pltpu.CompilerParams(
            collective_id=0, has_side_effects=True, vmem_limit_bytes=60 * 1024 * 1024
        ),
    )(wave_coef, diag_energy, left_block, right_block, block_mask)
    return (moved.reshape(width // 8, 8, cols) * scale).reshape(width, cols)


def solution(mesh):
    in_specs = (
        P("geom", "col"),
        P("geom", "col"),
        P(("geom", "op"), None, None),
        P(("geom", "op"), None, "col"),
        P(("geom", "op"), None, None),
    )
    return jax.shard_map(
        functools.partial(local, mesh.shape["op"] // 2, mesh.shape["col"]),
        mesh=mesh, in_specs=in_specs, out_specs=P("geom", "col"), check_vma=False,
    )
```

```python
import functools

import jax
import jax.numpy as jnp
from jax import lax
from jax.experimental import pallas as pl
from jax.experimental.pallas import tpu as pltpu
from jax.sharding import PartitionSpec as P

STEPS = 2
MESH = pl.DeviceIdType.MESH
F32 = jnp.float32
BF16 = jnp.bfloat16


def fold(total):
    return sum(total[:, i:i + 128] for i in range(0, total.shape[1], 128))


def whole(total):
    return jnp.sum(jnp.sum(total, axis=1, keepdims=True), axis=0, keepdims=True)


def rows8(product):
    return product.reshape(product.shape[0] // 8, 8, product.shape[1]).sum(0)


def kernel(
    groups, cells, wave_parts, tile,
    coef_hbm, diag_hbm, left_hbm, right_hbm, mask_ref,
    out_ref, norm_ref,
    coef, diag, left, right, masked, inner, wave_own, wave_other,
    own, y_out, y_in, z_out, z_in, sig, scal_out, scal_in,
    load_sem, wave_sem, y_sem, z_sem, zg_sem, yg_sem, scal_sem,
):
    op, col = lax.axis_index("op"), lax.axis_index("col")
    a, h = op // 2, lax.rem(op, 2)
    mate = a * 2 + 1 - h
    other = 1 - col
    width, cols = coef.shape
    pairs = left.shape[0]
    rows = width // (2 * groups)
    bands, band = inner.shape[0], inner.shape[2]
    blocks = mask_ref.shape[1]
    inside = width // blocks

    loads = [
        pltpu.make_async_copy(src, dst, load_sem.at[i])
        for i, (src, dst) in enumerate(
            ((coef_hbm, coef), (right_hbm, right), (left_hbm, left), (diag_hbm, diag))
        )
    ]
    for load in loads[:2]:
        load.start()

    barrier = pltpu.get_barrier_semaphore()
    peers = [{"col": other}, {"op": mate}]
    peers += [{"op": lax.rem(a + 1 + j, groups) * 2 + h} for j in range(groups - 1)]
    for peer in peers:
        pl.semaphore_signal(barrier, inc=1, device_id=peer, device_id_type=MESH)
    loads[0].wait()
    for load in loads[2:]:
        load.start()
    pl.semaphore_wait(barrier, len(peers))

    started = []

    def send(src, dst, sems, device_id):
        copy = pltpu.make_async_remote_copy(
            src_ref=src, dst_ref=dst, send_sem=sems[0], recv_sem=sems[1],
            device_id=device_id, device_id_type=MESH,
        )
        copy.start()
        started.append(copy)
        return copy

    def at(index):
        return pl.ds(pl.multiple_of(index * rows, rows), rows)

    def share(step, event, totals):
        for i, total in enumerate(totals):
            scal_out[step, event, i] = fold(total)
        copy = send(
            scal_out.at[step, event], scal_in.at[step, event],
            (scal_sem.at[0, step, event], scal_sem.at[1, step, event]), {"col": other},
        )
        copy.wait_recv()
        return [whole(scal_out[step, event, i] + scal_in[step, event, i]) for i in range(len(totals))]

    hops = (groups // 2, groups - 1 - groups // 2)
    legs = [(way, t) for t in range(hops[0]) for way in range(2) if t < hops[way]]

    def origin(way, t):
        return lax.rem(a + (groups - 1 - t if way == 0 else 1 + t), groups)

    ahead = sorted(range(1, groups), key=lambda d: -min(d, groups - d)) + [groups]

    def target_of(j):
        return lax.rem(a + ahead[j], groups)

    zero = jnp.zeros((8, cols), F32)
    scale = None
    for step in range(STEPS):
        part = width // wave_parts
        wave_copies = []
        for r in range(wave_parts):
            span = pl.ds(r * part, part)
            value = coef[span, :]
            if scale is not None:
                value = value * scale
                coef[span, :] = value
            wave_own[step, span, :] = value.astype(BF16)
            wave_copies.append(send(
                wave_own.at[step, span], wave_other.at[step, span],
                (wave_sem.at[0, step, r], wave_sem.at[1, step, r]), {"col": other},
            ))
        if step == 0:
            loads[1].wait()
        mine = pl.ds(pl.multiple_of(col * cols, cols), cols)
        theirs = pl.ds(pl.multiple_of(other * cols, cols), cols)
        state = {"corr": jnp.zeros((8, band), F32)}
        mate_in, group_in, mate_back, group_back = {}, {}, {}, {}

        def contract(b):
            lanes = slice(b * band, (b + 1) * band)
            for r in range(wave_parts):
                span = pl.ds(r * part, part)
                if b == 0:
                    wave_copies[r].wait_recv()
                for k in range(pairs):
                    value = jnp.dot(wave_own[step, span, :], right[k, mine, lanes], preferred_element_type=F32)
                    value += jnp.dot(wave_other[step, span, :], right[k, theirs, lanes], preferred_element_type=F32)
                    inner[b, pl.ds(k * width + r * part, part), :] = value.astype(BF16)

        def apply_mask():
            loads[2].wait()

            def mask_rows(i, carry):
                span = pl.ds(pl.multiple_of(i * inside, inside), inside)
                for k in range(pairs):
                    for j in range(blocks):
                        keep = jnp.full((inside, inside), mask_ref[k, i, j].astype(F32)).astype(BF16)
                        masked[span, k * width + j * inside:k * width + (j + 1) * inside] = (
                            left[k, span, j * inside:(j + 1) * inside] * keep
                        )
                return carry

            lax.fori_loop(0, blocks, mask_rows, 0)

        def halves(b):
            mate_in[b] = []
            for j in range(groups):
                target = target_of(j)
                span = pl.ds(pl.multiple_of(target * 2 * rows, 2 * rows), 2 * rows)
                value = jnp.dot(masked[span, :], inner[b], preferred_element_type=F32)
                low, high = value[:rows], value[rows:]
                y_out[step, b, j] = jnp.where(h == 0, high, low).astype(BF16)
                mate_in[b].append(send(
                    y_out.at[step, b, j], y_in.at[step, b, j],
                    (y_sem.at[0, step, b, j], y_sem.at[1, step, b, j]), {"op": mate},
                ))
                own[b, j] = jnp.where(h == 0, low, high)

        def to_owner(b):
            group_in[b] = []
            for j in range(groups):
                mate_in[b][j].wait_recv()
                value = own[b, j] + y_in[step, b, j].astype(F32)
                if j < groups - 1:
                    z_out[step, b, j] = value.astype(BF16)
                    group_in[b].append(send(
                        z_out.at[step, b, j], z_in.at[step, b, j],
                        (z_sem.at[0, step, b, j], z_sem.at[1, step, b, j]),
                        {"op": target_of(j) * 2 + h},
                    ))
                else:
                    own[b, j] = value

        def correlate(b, index):
            lanes = slice(b * band, (b + 1) * band)
            state["corr"] += rows8(coef[at(index), lanes] * sig[step, b, at(index), :].astype(F32))

        def relay(b, way, t, source):
            chunk = sig.at[step, b, at(source)]
            slot = way * hops[0] + t
            group_back[b, way, t] = send(
                chunk, chunk, (zg_sem.at[0, step, b, slot], zg_sem.at[1, step, b, slot]),
                {"op": lax.rem(a + (1 if way == 0 else groups - 1), groups) * 2 + h},
            )

        def finish(b):
            value = own[b, groups - 1]
            for j in range(groups - 1):
                group_in[b][j].wait_recv()
                value = value + z_in[step, b, j].astype(F32)
            sig[step, b, at(op), :] = value.astype(BF16)
            chunk = sig.at[step, b, at(op)]
            for way, length in enumerate(hops):
                if length:
                    relay(b, way, 0, op)
            mate_back[b] = [send(
                chunk, chunk,
                (yg_sem.at[0, step, b, groups - 1], yg_sem.at[1, step, b, groups - 1]), {"op": mate},
            )]
            correlate(b, op)

        def forward(b):
            for way, t in legs:
                group_back[b, way, t].wait_recv()
                source = origin(way, t) * 2 + h
                if t + 1 < hops[way]:
                    relay(b, way, t + 1, source)
                chunk = sig.at[step, b, at(source)]
                slot = way * hops[0] + t
                mate_back[b].append(send(
                    chunk, chunk, (yg_sem.at[0, step, b, slot], yg_sem.at[1, step, b, slot]), {"op": mate},
                ))
                correlate(b, source)

        def collect(b):
            mate_back[b][0].wait_recv()
            correlate(b, mate)
            for i, (way, t) in enumerate(legs):
                mate_back[b][1 + i].wait_recv()
                correlate(b, origin(way, t) * 2 + 1 - h)

        for b in range(bands):
            contract(b)
            if step == 0 and b == 0:
                apply_mask()
            halves(b)
        if step == 0:
            loads[3].wait()

        def weigh(i, acc):
            value = coef[pl.ds(pl.multiple_of(i * tile, tile), tile), :]
            return acc + rows8(value * value)

        weight = lax.fori_loop(0, width // tile, weigh, zero)
        for b in range(bands):
            to_owner(b)
            if b > 0:
                forward(b - 1)
            finish(b)
            if b > 0:
                collect(b - 1)
        forward(bands - 1)
        collect(bands - 1)
        correlation = state["corr"]

        total, weight = share(step, 0, [correlation, weight])
        theta = total / cells / (weight / cells + 1e-06)
        target_ref = coef if step < STEPS - 1 else out_ref

        def move(i, acc):
            span = pl.ds(pl.multiple_of(i * tile, tile), tile)
            value = coef[span, :]
            spacing = diag[span, :] - theta
            sigma = jnp.concatenate([sig[step, b, span, :] for b in range(bands)], axis=1).astype(F32)
            correction = (sigma - theta * value) * spacing * pl.reciprocal(jnp.maximum(spacing * spacing, 1.0))
            moved = value - correction
            target_ref[span, :] = moved
            return acc + rows8(moved * moved)

        norm = lax.fori_loop(0, width // tile, move, zero)
        (norm,) = share(step, 1, [norm])
        scale = lax.rsqrt(norm / cells + 1e-06)

    norm_ref[...] = jnp.broadcast_to(scale, norm_ref.shape)
    for copy in started:
        copy.wait_send()


def local(groups, sides, wave_coef, diag_energy, left_block, right_block, block_mask):
    width, cols = wave_coef.shape
    pairs = left_block.shape[0]
    rows = width // (2 * groups)
    parts = 4
    bands = max(1, cols // 256)
    band = cols // bands
    dma = pltpu.SemaphoreType.DMA
    vmem = pltpu.VMEM
    moved, scale = pl.pallas_call(
        functools.partial(kernel, groups, float(width * cols * sides), parts, 32),
        out_shape=(
            jax.ShapeDtypeStruct((width, cols), F32),
            jax.ShapeDtypeStruct((8, cols), F32),
        ),
        in_specs=[pl.BlockSpec(memory_space=pl.ANY)] * 4 + [pl.BlockSpec(memory_space=pltpu.SMEM)],
        out_specs=(pl.BlockSpec(memory_space=vmem), pl.BlockSpec(memory_space=vmem)),
        scratch_shapes=[
            vmem((width, cols), F32),
            vmem((width, cols), F32),
            vmem(left_block.shape, BF16),
            vmem(right_block.shape, BF16),
            vmem((width, pairs * width), BF16),
            vmem((bands, pairs * width, band), BF16),
            vmem((STEPS, width, cols), BF16),
            vmem((STEPS, width, cols), BF16),
            vmem((bands, groups, rows, band), F32),
            vmem((STEPS, bands, groups, rows, band), BF16),
            vmem((STEPS, bands, groups, rows, band), BF16),
            vmem((STEPS, bands, groups - 1, rows, band), BF16),
            vmem((STEPS, bands, groups - 1, rows, band), BF16),
            vmem((STEPS, bands, width, band), BF16),
            vmem((STEPS, 2, 2, 8, 128), F32),
            vmem((STEPS, 2, 2, 8, 128), F32),
            dma((4,)),
            dma((2, STEPS, parts)),
            dma((2, STEPS, bands, groups)),
            dma((2, STEPS, bands, groups - 1)),
            dma((2, STEPS, bands, groups - 1)),
            dma((2, STEPS, bands, groups)),
            dma((2, STEPS, 2)),
        ],
        compiler_params=pltpu.CompilerParams(
            collective_id=0, has_side_effects=True, vmem_limit_bytes=60 * 1024 * 1024
        ),
    )(wave_coef, diag_energy, left_block, right_block, block_mask)
    return (moved.reshape(width // 8, 8, cols) * scale).reshape(width, cols)


def solution(mesh):
    in_specs = (
        P("geom", "col"),
        P("geom", "col"),
        P(("geom", "op"), None, None),
        P(("geom", "op"), None, "col"),
        P(("geom", "op"), None, None),
    )
    return jax.shard_map(
        functools.partial(local, mesh.shape["op"] // 2, mesh.shape["col"]),
        mesh=mesh, in_specs=in_specs, out_specs=P("geom", "col"), check_vma=False,
    )
```
